256 devices in a mesh: batch: 128 (over z, y_lo, x, core), crop: 2 (over y_hi).
Axes of the slice: x: 4, y: 4 (y_hi: 2, y_lo: 2; y = y_hi * 2 + y_lo), z: 8, core: 2. Of those that a mesh axis runs over, the one named last changes fastest.
Arguments:
- voxels: bfloat16 [2, 131072, 512], P('crop', 'batch'), may hold values from -6 to 6
- phrases: bfloat16 [2048, 512], P('batch'), may hold values from -6 to 6
- pair_ids: int32 [2048], P('batch'), may hold values from 0 to 511
- margin_index: int32 [2, 128, 512], P('crop', 'batch'), may hold values from 0 to 1023, as said below
Outputs:
- voxel_grad: float32 [2, 131072, 512], P('crop', 'batch')
- phrase_grad: float32 [2048, 512], P('batch')
The draws below stay inside these ranges and needn't reach their ends.
Inputs may be any that keep to these rules, and one draw needn't show every extreme that they name: Each list margin_index[c, b] holds 512 distinct rows of that batch index's 1024 rows; entry k of crop 0 and entry k of crop 1 at the same b show the same place.
All inputs are finite; a program needn't handle non-finite values.
Results may differ from the reference program's by a relative error of at most 0.0013.
Values may be sent and summed in bfloat16 or wider, within the bound.
A program may use at most 64 MiB of HBM per device.

```python
import math
import jax
import jax.numpy as jnp
from jax import lax

D = 512
VOX_DEV = 1024
VOX_VOL = 256
OVL = 512
VOXELS = 131072
PHRASES = 2048
VOLUMES = 512
N_BATCH = 128


def draw_margin_index(key, part):
    keys = jax.random.split(key, 2 * N_BATCH)

    def one_list(single):
        return jax.random.permutation(single, VOX_DEV)[:OVL].astype(jnp.int32)
    lists = jax.vmap(one_list)(keys)
    return lists.reshape(2, N_BATCH, OVL)


def set_ends(entries, own_key, least, top_value):
    shape = entries.shape
    index_at = [jax.random.randint(jax.random.fold_in(own_key, axis), (), 0, shape[axis]) for axis in range(len(shape))]
    entries = entries.at[tuple(index_at)].set(least)
    longest = shape.index(max(shape))
    index_at[longest] = (index_at[longest] + 1) % shape[longest]
    return entries.at[tuple(index_at)].set(top_value)


def block_levels(key, extent, cuts, least, high):
    level, own = 1.0, jax.random.fold_in(key, 6)
    for dim, shards_of in cuts:
        draws = jnp.exp(jax.random.uniform(jax.random.fold_in(own, dim), (shards_of,), jnp.float32, least / len(cuts), high / len(cuts)))
        level = level * jnp.repeat(draws, extent[dim] // shards_of).reshape([-1 if axis == dim else 1 for axis in range(len(extent))])
    return level


def gaussian(key, shape, spread, bound, cuts=(), held_as=jnp.bfloat16):
    gain = block_levels(key, shape, cuts, -0.22, 0.18) if cuts else 1.0
    result = jax.random.normal(key, shape, jnp.float32) * spread * gain
    return jnp.minimum(jnp.maximum(result, -bound), bound).astype(held_as)


def setup_inputs(seed: int = 0) -> dict:
    key_list = jax.random.split(jax.random.key(seed), 5)
    return {
        "voxels": gaussian(key_list[0], (2, VOXELS, D), 1.0, 6.0, ((0, 2), (1, 128))),
        "phrases": gaussian(key_list[1], (PHRASES, D), 1.0, 6.0, ((0, 128),)),
        "pair_ids": set_ends(jax.random.randint(key_list[2], (PHRASES,), 0, VOLUMES), jax.random.fold_in(key_list[2], 1), 0, VOLUMES - 1).astype(jnp.int32),
        "margin_index": draw_margin_index(jax.random.fold_in(key_list[4], 71), 0),
    }


def reference(voxels, phrases, pair_ids, margin_index):
    scale = 1.0 / math.sqrt(D)
    all_rows = voxels.reshape(2 * VOXELS, D)
    block_rows = math.gcd(2 * VOXELS, 2048)
    num_blocks = 2 * VOXELS // block_rows
    blocks = all_rows.reshape(num_blocks, block_rows, D)
    starts = jnp.arange(num_blocks, dtype=jnp.int32) * block_rows

    def one_block(total, pieces):
        group, start = pieces
        index = start + jnp.arange(block_rows, dtype=jnp.int32)
        volume = index % VOXELS // VOX_VOL
        sign = jnp.where(volume[:, None] == pair_ids[None, :], 1.0, -1.0).astype(jnp.float32)
        logit = jnp.dot(group, phrases.T, preferred_element_type=jnp.float32) * scale - 1.0
        dlogit = (-sign * jax.nn.sigmoid(-sign * logit)).astype(jnp.bfloat16)
        match_part = jnp.dot(dlogit, phrases, preferred_element_type=jnp.float32) * scale
        phrase_part = jnp.dot(dlogit.T, group, preferred_element_type=jnp.float32) * scale
        return (total + phrase_part, match_part)
    phrase_grad, match_blocks = lax.scan(one_block, jnp.zeros((PHRASES, D), jnp.float32), (blocks, starts))
    match_grad = match_blocks.reshape(2, VOXELS, D)
    base = (jnp.arange(N_BATCH, dtype=jnp.int32) * VOX_DEV)[:, None]
    rows_first = (base + margin_index[0].astype(jnp.int32)).reshape(-1)
    rows_second = (base + margin_index[1].astype(jnp.int32)).reshape(-1)
    first = voxels[0][rows_first].astype(jnp.float32)
    second = voxels[1][rows_second].astype(jnp.float32)
    diff = first - second
    grad_first = match_grad[0].at[rows_first].add(diff)
    grad_second = match_grad[1].at[rows_second].add(-diff)
    voxel_grad = jnp.stack([grad_first, grad_second])
    return (voxel_grad, phrase_grad)
```

```python
import math

import jax
import jax.numpy as jnp
from jax import lax
from jax.experimental import pallas as pl
from jax.experimental.pallas import tpu as pltpu
from jax.sharding import PartitionSpec as P

MESH = pl.DeviceIdType.MESH
F32, BF16 = jnp.float32, jnp.bfloat16
NT = (((1,), (1,)), ((), ()))
TN = (((0,), (0,)), ((), ()))
VOX_VOL = 256
NX, NY, NZ = 4, 4, 8
OFFS = (0, 1, -1, 2, -2, 3, -3, 4)
BACK = tuple(OFFS.index(-o if o != 4 else 4) for o in OFFS)
GROUPS = ((0, 1), (1, 1), (2, 2), (4, 2), (6, 2))
PLANE = tuple(
    sorted(
        ((dx, dy) for dx in range(NX) for dy in range(NY) if (dx, dy) != (0, 0)),
        key=lambda d: -(min(d[0], NX - d[0]) + min(d[1], NY - d[1])),
    )
)
MARGIN_CHUNKS = 8
NUM_SEMS = 192


def kernel(
    vox_in, phr_in, ids_in, mrg_in, vg_out, pg_out,
    vx, ph, idb, idr, dt, st, ch, part, sb, rb, zs, zr, fs, fr, ms, mr, mo, vg,
    send_sem, recv_sem, loc_sem,
):
    rows, width = vox_in.shape
    own = phr_in.shape[0]
    half = width // 2
    scale = 1.0 / math.sqrt(width)
    b, c = lax.axis_index("batch"), lax.axis_index("crop")
    k, x, ylo, z = b % 2, (b // 2) % 4, (b // 8) % 2, b // 16
    y = c * 2 + ylo
    g, go = ylo * 4 + x, (1 - ylo) * 4 + x

    def at(dx=0, dy=0, dz=0, dk=0):
        xx, yy, zz, kk = (x + dx) % NX, (y + dy) % NY, (z + dz + NZ) % NZ, (k + dk) % 2
        return (((zz * 2 + yy % 2) * 4 + xx) * 2 + kk, yy // 2)

    count = [0]
    started = []

    def send(src, dst, where):
        n = count[0]
        count[0] += 1
        copy = pltpu.make_async_remote_copy(
            src_ref=src, dst_ref=dst, send_sem=send_sem.at[n], recv_sem=recv_sem.at[n],
            device_id=where, device_id_type=MESH,
        )
        copy.start()
        started.append(copy)
        return copy

    barrier = pltpu.get_barrier_semaphore()
    partners = [dict(dk=1)]
    partners += [dict(dz=o) for o in OFFS[1:]]
    partners += [dict(dx=dx, dy=dy) for dx, dy in PLANE]
    for p in partners:
        pl.semaphore_signal(barrier, inc=1, device_id=at(**p), device_id_type=MESH)

    mine = pl.ds(pl.multiple_of(k * rows, rows), rows)
    theirs = pl.ds(pl.multiple_of((1 - k) * rows, rows), rows)
    load_vox = pltpu.make_async_copy(vox_in, vx.at[mine], loc_sem.at[0])
    load_vox.start()
    load_phr = pltpu.make_async_copy(phr_in, ph.at[0, g], loc_sem.at[1])
    load_phr.start()
    idr[...] = jnp.zeros_like(idr)
    idr[:, 0:own] = ids_in[...]
    st[...] = (lax.broadcasted_iota(jnp.int32, st.shape, 0) == mrg_in[...]).astype(F32).astype(BF16)
    load_vox.wait()
    ch[...] = lax.dot_general(st[...], vx[mine, :], TN, preferred_element_type=F32).astype(BF16)
    load_phr.wait()
    idb[g, 0] = idr[...]
    pl.semaphore_wait(barrier, len(partners))

    margin = []
    step = ch.shape[0] // MARGIN_CHUNKS

    def send_margin(n):
        for _ in range(n):
            i = len(margin)
            if i < MARGIN_CHUNKS:
                piece = pl.ds(i * step, step)
                margin.append(send(ch.at[piece], part.at[piece], at(dy=2)))

    def forward(n, start, which):
        return [
            send(ph.at[pl.ds(start, n), which], ph.at[pl.ds(start, n), which], at(dx=dx))
            for dx in (2, 1, 3)
        ]

    def across(n, start):
        lo, hi = pl.ds(0, half), pl.ds(half, half)
        s = pl.ds(start, n)
        return [
            send(ph.at[s, g, :, lo], ph.at[s, g, :, lo], at(dy=1)),
            send(ph.at[s, g, :, hi], ph.at[s, g, :, hi], at(dy=3)),
        ]

    zc = {}
    for p in (7, 5, 6, 3, 4, 1, 2):
        zc[p] = send(phr_in, ph.at[BACK[p], g], at(dz=OFFS[p]))
    same, cross, other = [], [], []
    cross.append(across(1, 0))
    same.append(forward(1, 0, g))
    swap_vox = send(vox_in, vx.at[mine], at(dk=1))
    idc = {p: send(idr, idb.at[g, BACK[p]], at(dz=OFFS[p])) for p in range(1, NZ)}
    send_margin(1)
    for i, (start, n) in enumerate(GROUPS):
        if i == 0:
            continue
        for q in range(start, start + n):
            zc[BACK[q]].wait_recv()
        cross.append(across(n, start))
        same.append(forward(n, start, g))
        send_margin(2)
        for copy in cross[i - 1]:
            copy.wait_recv()
        pstart, pn = GROUPS[i - 1]
        other.append(forward(pn, pstart, go))
    for p in range(1, NZ):
        idc[p].wait_recv()
    id_y = send(idb.at[g], idb.at[g], at(dy=1 + 2 * ylo))
    id_same = [send(idb.at[g], idb.at[g], at(dx=dx)) for dx in (2, 1, 3)]
    for copy in cross[-1]:
        copy.wait_recv()
    pstart, pn = GROUPS[-1]
    other.append(forward(pn, pstart, go))
    id_y.wait_recv()
    id_other = [send(idb.at[go], idb.at[go], at(dx=dx)) for dx in (2, 1, 3)]
    send_margin(MARGIN_CHUNKS)
    swap_vox.wait_recv()
    for copy in id_same + id_other:
        copy.wait_recv()

    chunk = 1024
    total = vx.shape[0]
    first_vol = (b // 2) * (total // VOX_VOL)
    lane = lax.broadcasted_iota(jnp.int32, (128, 128), 1)
    row16 = lax.broadcasted_iota(jnp.int32, (128, 128), 0) % own
    pick = lane == row16

    def logits(i):
        for q, (start, n) in enumerate(GROUPS):
            if start // 2 == i:
                for copy in same[q] + other[q]:
                    copy.wait_recv()
        block = ph[2 * i : 2 * i + 2].reshape(256, width)
        cols = []
        for j in range(2):
            ids = jnp.broadcast_to(idb[:, 2 * i + j], (8, own, 128)).reshape(128, 128)
            cols.append(jnp.sum(jnp.where(pick, ids, 0).astype(F32), axis=1, keepdims=True))
        ids = jnp.concatenate(cols, axis=0)
        for t in range(total // chunk):
            c0 = t * chunk
            acc = lax.dot_general(block, vx[c0 : c0 + chunk, :], NT, preferred_element_type=F32)
            logit = acc * scale - 1.0
            vol = first_vol + (c0 + lax.broadcasted_iota(jnp.int32, (1, chunk), 1)) // VOX_VOL
            match = ids == vol.astype(F32)
            r = 1.0 / (1.0 + jnp.exp(jnp.where(match, logit, -logit)))
            dt[i * 256 : (i + 1) * 256, c0 : c0 + chunk] = jnp.where(match, -r, r).astype(BF16)

    pieces = {}

    def terms(i):
        r = jnp.dot(dt[i * 256 : (i + 1) * 256, :], vx[...], preferred_element_type=F32).astype(BF16)
        for gg in range(8):
            for h in range(2):
                for j in range(2):
                    r0 = j * 128 + gg * own
                    sb[i, gg, h, j] = r[r0 : r0 + own, h * half : (h + 1) * half]

    def send_terms(i):
        copies = []
        for n, (dx, dy) in enumerate(PLANE):
            yy = (y + dy) % NY
            gg = (yy % 2) * 4 + (x + dx) % NX
            copies.append(send(sb.at[i, gg, yy // 2], rb.at[i, n], at(dx=dx, dy=dy)))
        pieces[i] = copies

    zsum = {}

    def collect(i):
        for copy in pieces[i]:
            copy.wait_recv()
        acc = sb[i, g, c].astype(F32)
        for n in range(len(PLANE)):
            acc = acc + rb[i, n].astype(F32)
        zs[2 * i : 2 * i + 2] = acc
        for p in (2 * i, 2 * i + 1):
            if p:
                zsum[p] = send(zs.at[p], zr.at[BACK[p]], at(dz=OFFS[p]))

    logits(0)
    logits(1)
    terms(1)
    logits(2)
    send_terms(1)
    terms(2)
    logits(3)
    send_terms(2)
    terms(3)
    terms(0)
    send_terms(3)
    send_terms(0)

    flat = ph[...].reshape(NZ * 128, width)
    mstep = 512
    swaps = []
    for t in range(rows // mstep):
        cols = pl.ds(pl.multiple_of((1 - k) * rows + t * mstep, mstep), mstep)
        piece = pl.ds(t * mstep, mstep)
        ms[piece, :] = lax.dot_general(dt[:, cols], flat, TN, preferred_element_type=F32)
    for t in range(rows // mstep):
        piece = pl.ds(t * mstep, mstep)
        swaps.append(send(ms.at[piece], mr.at[piece], at(dk=1)))
    collect(1)
    for t in range(rows // mstep):
        cols = pl.ds(pl.multiple_of(k * rows + t * mstep, mstep), mstep)
        piece = pl.ds(t * mstep, mstep)
        mo[piece, :] = lax.dot_general(dt[:, cols], flat, TN, preferred_element_type=F32)
    collect(2)
    for copy in margin:
        copy.wait_recv()
    for copy in swaps:
        copy.wait_recv()
    fstep = 256
    stores = []
    for t in range(rows // fstep):
        piece = pl.ds(t * fstep, fstep)
        sel = st[piece, :]
        held = jnp.sum(sel.astype(F32), axis=1, keepdims=True)
        lower = pl.ds(pl.multiple_of(k * rows + t * fstep, fstep), fstep)
        extra = vx[lower, :].astype(F32) * held - jnp.dot(sel, part[...], preferred_element_type=F32)
        vg[piece, :] = (mo[piece, :] + mr[piece, :]) * scale + extra
    for t in range(rows // fstep):
        piece = pl.ds(t * fstep, fstep)
        store = pltpu.make_async_copy(vg.at[piece], vg_out.at[piece], loc_sem.at[2 + t])
        store.start()
        stores.append(store)
    collect(3)
    collect(0)
    acc = zs[0]
    for p in (7, 6, 5, 4, 3, 2, 1):
        zsum[p].wait_recv()
        acc = acc + zr[BACK[p]]
    fs[...] = acc * scale
    last = send(fs, fr, at(dy=2))
    for store in stores:
        store.wait()
    last.wait_recv()
    a, d = fs[...], fr[...]
    pg_out[:, 0:half] = jnp.where(c == 0, a, d)
    pg_out[:, half:width] = jnp.where(c == 0, d, a)
    for copy in started:
        copy.wait_send()
    assert count[0] <= NUM_SEMS


def local(voxels, phrases, pair_ids, margin_index):
    rows, width = voxels.shape[1:]
    own = phrases.shape[0]
    ovl = margin_index.shape[-1]
    half = width // 2
    vmem = pl.BlockSpec(memory_space=pltpu.VMEM)
    hbm = pl.BlockSpec(memory_space=pl.ANY)
    voxel_grad, phrase_grad = pl.pallas_call(
        kernel,
        name="grounding",
        out_shape=(
            jax.ShapeDtypeStruct((rows, width), F32),
            jax.ShapeDtypeStruct((own, width), F32),
        ),
        in_specs=[hbm, hbm, vmem, vmem],
        out_specs=(hbm, vmem),
        scratch_shapes=[
            pltpu.VMEM((2 * rows, width), BF16),
            pltpu.VMEM((NZ, 8, own, width), BF16),
            pltpu.VMEM((8, NZ, 1, 128), jnp.int32),
            pltpu.VMEM((1, 128), jnp.int32),
            pltpu.VMEM((NZ * 8 * own, 2 * rows), BF16),
            pltpu.VMEM((rows, ovl), BF16),
            pltpu.VMEM((ovl, width), BF16),
            pltpu.VMEM((ovl, width), BF16),
            pltpu.VMEM((4, 8, 2, 2, own, half), BF16),
            pltpu.VMEM((4, 15, 2, own, half), BF16),
            pltpu.VMEM((NZ, own, half), F32),
            pltpu.VMEM((NZ, own, half), F32),
            pltpu.VMEM((own, half), F32),
            pltpu.VMEM((own, half), F32),
            pltpu.VMEM((rows, width), F32),
            pltpu.VMEM((rows, width), F32),
            pltpu.VMEM((rows, width), F32),
            pltpu.VMEM((rows, width), F32),
            pltpu.SemaphoreType.DMA((NUM_SEMS,)),
            pltpu.SemaphoreType.DMA((NUM_SEMS,)),
            pltpu.SemaphoreType.DMA((8,)),
        ],
        compiler_params=pltpu.CompilerParams(
            collective_id=0, has_side_effects=True, vmem_limit_bytes=56 * 2**20
        ),
    )(voxels[0], phrases, pair_ids[None], margin_index[0])
    return (voxel_grad[None], phrase_grad)


def solution(mesh):
    placed = (P("crop", "batch", None), P("batch", None), P("batch"), P("crop", "batch", None))
    return jax.shard_map(
        local,
        mesh=mesh,
        in_specs=placed,
        out_specs=(P("crop", "batch", None), P("batch", None)),
        check_vma=False,
    )
```

```python
import math

import jax
import jax.numpy as jnp
from jax import lax
from jax.experimental import pallas as pl
from jax.experimental.pallas import tpu as pltpu
from jax.sharding import PartitionSpec as P

MESH = pl.DeviceIdType.MESH
F32, BF16 = jnp.float32, jnp.bfloat16
NT = (((1,), (1,)), ((), ()))
TN = (((0,), (0,)), ((), ()))
VOX_VOL = 256
NX, NY, NZ = 4, 4, 8
OFFS = (0, 1, -1, 2, -2, 3, -3, 4)
BACK = tuple(OFFS.index(-o if o != 4 else 4) for o in OFFS)
GROUPS = ((0, 1), (1, 1), (2, 2), (4, 2), (6, 2))
PLANE = tuple(
    sorted(
        ((dx, dy) for dx in range(NX) for dy in range(NY) if (dx, dy) != (0, 0)),
        key=lambda d: -(min(d[0], NX - d[0]) + min(d[1], NY - d[1])),
    )
)
MARGIN_CHUNKS = 8
EARLY = 1
LATER = 1
NUM_SEMS = 192


def kernel(
    vox_in, phr_in, ids_in, mrg_in, vg_out, pg_out,
    vx, ph, idb, idr, dt, st, ch, part, sb, rb, zs, zr, fs, fr, ms, mr, mo, vg, idv, mrv, pg, fn,
    send_sem, recv_sem, loc_sem,
):
    rows, width = vox_in.shape
    own = phr_in.shape[0]
    half = width // 2
    scale = 1.0 / math.sqrt(width)
    b, c = lax.axis_index("batch"), lax.axis_index("crop")
    k, x, ylo, z = b % 2, (b // 2) % 4, (b // 8) % 2, b // 16
    y = c * 2 + ylo
    g, go = ylo * 4 + x, (1 - ylo) * 4 + x

    def at(dx=0, dy=0, dz=0, dk=0):
        xx, yy, zz, kk = (x + dx) % NX, (y + dy) % NY, (z + dz + NZ) % NZ, (k + dk) % 2
        return (((zz * 2 + yy % 2) * 4 + xx) * 2 + kk, yy // 2)

    count = [0]
    started = []

    def send(src, dst, where):
        n = count[0]
        count[0] += 1
        copy = pltpu.make_async_remote_copy(
            src_ref=src, dst_ref=dst, send_sem=send_sem.at[n], recv_sem=recv_sem.at[n],
            device_id=where, device_id_type=MESH,
        )
        copy.start()
        started.append(copy)
        return copy

    barrier = pltpu.get_barrier_semaphore()
    partners = [dict(dk=1)]
    partners += [dict(dz=o) for o in OFFS[1:]]
    partners += [dict(dx=dx, dy=dy) for dx, dy in PLANE]
    partners += [dict(dy=2, dz=1), dict(dy=2, dz=-1)]
    for p in partners:
        pl.semaphore_signal(barrier, inc=1, device_id=at(**p), device_id_type=MESH)

    mine = pl.ds(pl.multiple_of(k * rows, rows), rows)
    theirs = pl.ds(pl.multiple_of((1 - k) * rows, rows), rows)
    load_vox = pltpu.make_async_copy(vox_in, vx.at[mine], loc_sem.at[0])
    load_vox.start()
    load_phr = pltpu.make_async_copy(phr_in, ph.at[0, g], loc_sem.at[1])
    load_phr.start()
    load_ids = pltpu.make_async_copy(ids_in, idv, loc_sem.at[6])
    load_ids.start()
    load_mrg = pltpu.make_async_copy(mrg_in, mrv, loc_sem.at[7])
    load_mrg.start()
    load_ids.wait()
    idr[...] = jnp.zeros_like(idr)
    idr[:, 0:own] = idv[...]
    load_mrg.wait()
    st[...] = (lax.broadcasted_iota(jnp.int32, st.shape, 0) == mrv[...]).astype(F32).astype(BF16)
    load_vox.wait()
    ch[...] = lax.dot_general(st[...], vx[mine, :], TN, preferred_element_type=F32).astype(BF16)
    load_phr.wait()
    idb[g, 0] = idr[...]
    pl.semaphore_wait(barrier, len(partners))

    margin = []
    step = ch.shape[0] // MARGIN_CHUNKS

    def send_margin(n):
        for _ in range(n):
            i = len(margin)
            if i < MARGIN_CHUNKS:
                piece = pl.ds(i * step, step)
                margin.append(send(ch.at[piece], part.at[piece], at(dy=2)))

    def forward(n, start, which):
        return [
            send(ph.at[pl.ds(start, n), which], ph.at[pl.ds(start, n), which], at(dx=dx))
            for dx in (2, 1, 3)
        ]

    def across(n, start):
        lo, hi = pl.ds(0, half), pl.ds(half, half)
        s = pl.ds(start, n)
        return [
            send(ph.at[s, g, :, lo], ph.at[s, g, :, lo], at(dy=1)),
            send(ph.at[s, g, :, hi], ph.at[s, g, :, hi], at(dy=3)),
        ]

    zc = {}
    idc = {p: send(idr, idb.at[g, BACK[p]], at(dz=OFFS[p])) for p in range(1, NZ)}
    for p in (7, 5, 6, 3, 4, 1, 2):
        zc[p] = send(phr_in, ph.at[BACK[p], g], at(dz=OFFS[p]))
    same, cross, other = [], [], []
    cross.append(across(1, 0))
    same.append(forward(1, 0, g))
    swap_vox = send(vox_in, vx.at[mine], at(dk=1))
    send_margin(EARLY)

    def relay(i):
        start, n = GROUPS[i]
        for q in range(start, start + n):
            zc[BACK[q]].wait_recv()
        cross.append(across(n, start))
        same.append(forward(n, start, g))

    def relay_other(i):
        start, n = GROUPS[i]
        for copy in cross[i]:
            copy.wait_recv()
        other.append(forward(n, start, go))

    relay(1)
    relay_other(0)
    for p in range(1, NZ):
        idc[p].wait_recv()
    beside = 1 + 2 * ylo
    ids_seen = [send(idb.at[g], idb.at[g], at(dx=dx, dy=beside)) for dx in (2, 1, 3, 0)]
    ids_seen += [send(idb.at[g], idb.at[g], at(dx=dx)) for dx in (2, 1, 3)]
    for i in (2, 3, 4):
        relay(i)
        relay_other(i - 1)
        send_margin(LATER)

    chunk = 1024
    total = vx.shape[0]
    first_vol = (b // 2) * (total // VOX_VOL)
    lane = lax.broadcasted_iota(jnp.int32, (128, 128), 1)
    row16 = lax.broadcasted_iota(jnp.int32, (128, 128), 0) % own
    pick = lane == row16

    def logits(i):
        for q, (start, n) in enumerate(GROUPS):
            if start // 2 == i:
                for copy in same[q] + other[q]:
                    copy.wait_recv()
        block = ph[2 * i : 2 * i + 2].reshape(256, width)
        cols = []
        for j in range(2):
            ids = jnp.broadcast_to(idb[:, 2 * i + j], (8, own, 128)).reshape(128, 128)
            cols.append(jnp.sum(jnp.where(pick, ids, 0).astype(F32), axis=1, keepdims=True))
        ids = jnp.concatenate(cols, axis=0)
        for t in range(total // chunk):
            c0 = t * chunk
            acc = lax.dot_general(block, vx[c0 : c0 + chunk, :], NT, preferred_element_type=F32)
            logit = acc * scale - 1.0
            vol = first_vol + (c0 + lax.broadcasted_iota(jnp.int32, (1, chunk), 1)) // VOX_VOL
            match = ids == vol.astype(F32)
            r = 1.0 / (1.0 + jnp.exp(jnp.where(match, logit, -logit)))
            dt[i * 256 : (i + 1) * 256, c0 : c0 + chunk] = jnp.where(match, -r, r).astype(BF16)

    pieces = {}

    def terms(i):
        r = jnp.dot(dt[i * 256 : (i + 1) * 256, :], vx[...], preferred_element_type=F32).astype(BF16)
        for gg in range(8):
            for h in range(2):
                for j in range(2):
                    r0 = j * 128 + gg * own
                    sb[i, gg, h, j] = r[r0 : r0 + own, h * half : (h + 1) * half]

    def send_terms(i):
        copies = []
        for n, (dx, dy) in enumerate(PLANE):
            yy = (y + dy) % NY
            gg = (yy % 2) * 4 + (x + dx) % NX
            copies.append(send(sb.at[i, gg, yy // 2], rb.at[i, n], at(dx=dx, dy=dy)))
        pieces[i] = copies

    zsum, near = {}, []

    def collect(i):
        for copy in pieces[i]:
            copy.wait_recv()
        acc = sb[i, g, c].astype(F32)
        for n in range(len(PLANE)):
            acc = acc + rb[i, n].astype(F32)
        zs[2 * i : 2 * i + 2] = acc
        for p in (2 * i, 2 * i + 1):
            if p:
                zsum[p] = send(zs.at[p], zr.at[BACK[p]], at(dz=OFFS[p]))
            if p == 1:
                near.append(send(zs.at[p], fn, at(dy=2, dz=1)))

    swap_vox.wait_recv()
    for copy in ids_seen:
        copy.wait_recv()
    logits(0)
    relay_other(4)
    send_margin(MARGIN_CHUNKS)
    logits(1)
    terms(1)
    logits(2)
    send_terms(1)
    terms(2)
    logits(3)
    send_terms(2)
    terms(3)
    terms(0)
    send_terms(3)
    send_terms(0)

    flat = ph[...].reshape(NZ * 128, width)
    mstep = 512
    swaps = []
    for t in range(rows // mstep):
        cols = pl.ds(pl.multiple_of((1 - k) * rows + t * mstep, mstep), mstep)
        piece = pl.ds(t * mstep, mstep)
        ms[piece, :] = lax.dot_general(dt[:, cols], flat, TN, preferred_element_type=F32)
    for t in range(rows // mstep):
        piece = pl.ds(t * mstep, mstep)
        swaps.append(send(ms.at[piece], mr.at[piece], at(dk=1)))
    collect(1)
    for t in range(rows // mstep):
        cols = pl.ds(pl.multiple_of(k * rows + t * mstep, mstep), mstep)
        piece = pl.ds(t * mstep, mstep)
        mo[piece, :] = lax.dot_general(dt[:, cols], flat, TN, preferred_element_type=F32)
    collect(2)
    for copy in margin:
        copy.wait_recv()
    for copy in swaps:
        copy.wait_recv()
    fstep = 256
    stores = []
    for t in range(rows // fstep):
        piece = pl.ds(t * fstep, fstep)
        sel = st[piece, :]
        held = jnp.sum(sel.astype(F32), axis=1, keepdims=True)
        lower = pl.ds(pl.multiple_of(k * rows + t * fstep, fstep), fstep)
        extra = vx[lower, :].astype(F32) * held - jnp.dot(sel, part[...], preferred_element_type=F32)
        vg[piece, :] = (mo[piece, :] + mr[piece, :]) * scale + extra
    for t in range(rows // fstep):
        piece = pl.ds(t * fstep, fstep)
        store = pltpu.make_async_copy(vg.at[piece], vg_out.at[piece], loc_sem.at[2 + t])
        store.start()
        stores.append(store)
    collect(3)
    collect(0)
    acc = zs[0]
    for p in (7, 6, 5, 4, 3, 2):
        zsum[p].wait_recv()
        acc = acc + zr[BACK[p]]
    fs[...] = acc
    last = send(fs, fr, at(dy=2))
    zsum[1].wait_recv()
    for store in stores:
        store.wait()
    last.wait_recv()
    near[0].wait_recv()
    a, d = (fs[...] + zr[BACK[1]]) * scale, (fr[...] + fn[...]) * scale
    pg[:, 0:half] = jnp.where(c == 0, a, d)
    pg[:, half:width] = jnp.where(c == 0, d, a)
    store = pltpu.make_async_copy(pg, pg_out, loc_sem.at[8])
    store.start()
    store.wait()
    for copy in started:
        copy.wait_send()
    assert count[0] <= NUM_SEMS


def local(voxels, phrases, pair_ids, margin_index):
    rows, width = voxels.shape[1:]
    own = phrases.shape[0]
    ovl = margin_index.shape[-1]
    half = width // 2
    hbm = pl.BlockSpec(memory_space=pltpu.HBM)
    any_space = pl.BlockSpec(memory_space=pl.ANY)
    inputs = (voxels[0], phrases, pair_ids[None], margin_index[0])
    voxel_grad, phrase_grad = pl.pallas_call(
        kernel,
        name="grounding",
        out_shape=(
            jax.ShapeDtypeStruct((rows, width), F32),
            jax.ShapeDtypeStruct((own, width), F32),
        ),
        in_specs=[hbm, hbm, hbm, hbm],
        out_specs=(any_space, any_space),
        scratch_shapes=[
            pltpu.VMEM((2 * rows, width), BF16),
            pltpu.VMEM((NZ, 8, own, width), BF16),
            pltpu.VMEM((8, NZ, 1, 128), jnp.int32),
            pltpu.VMEM((1, 128), jnp.int32),
            pltpu.VMEM((NZ * 8 * own, 2 * rows), BF16),
            pltpu.VMEM((rows, ovl), BF16),
            pltpu.VMEM((ovl, width), BF16),
            pltpu.VMEM((ovl, width), BF16),
            pltpu.VMEM((4, 8, 2, 2, own, half), BF16),
            pltpu.VMEM((4, 15, 2, own, half), BF16),
            pltpu.VMEM((NZ, own, half), F32),
            pltpu.VMEM((NZ, own, half), F32),
            pltpu.VMEM((own, half), F32),
            pltpu.VMEM((own, half), F32),
            pltpu.VMEM((rows, width), F32),
            pltpu.VMEM((rows, width), F32),
            pltpu.VMEM((rows, width), F32),
            pltpu.VMEM((rows, width), F32),
            pltpu.VMEM((1, own), jnp.int32),
            pltpu.VMEM((1, ovl), jnp.int32),
            pltpu.VMEM((own, width), F32),
            pltpu.VMEM((own, half), F32),
            pltpu.SemaphoreType.DMA((NUM_SEMS,)),
            pltpu.SemaphoreType.DMA((NUM_SEMS,)),
            pltpu.SemaphoreType.DMA((16,)),
        ],
        compiler_params=pltpu.CompilerParams(
            collective_id=0, has_side_effects=True, vmem_limit_bytes=24 * 2**20
        ),
    )(*(pltpu.with_memory_space_constraint(a, pltpu.HBM) for a in inputs))
    return (voxel_grad[None], phrase_grad)


def solution(mesh):
    placed = (P("crop", "batch", None), P("batch", None), P("batch"), P("crop", "batch", None))
    return jax.shard_map(
        local,
        mesh=mesh,
        in_specs=placed,
        out_specs=(P("crop", "batch", None), P("batch", None)),
        check_vma=False,
    )
```

```python
import math

import jax
import jax.numpy as jnp
from jax import lax
from jax.experimental import pallas as pl
from jax.experimental.pallas import tpu as pltpu
from jax.sharding import PartitionSpec as P

MESH = pl.DeviceIdType.MESH
F32, BF16 = jnp.float32, jnp.bfloat16
NT = (((1,), (1,)), ((), ()))
TN = (((0,), (0,)), ((), ()))
VOX_VOL = 256
NX, NY, NZ = 4, 4, 8
OFFS = (0, -2, 1, -1, 3, 4, 2, -3)
BACK = tuple(OFFS.index(-o if o != 4 else 4) for o in OFFS)
GROUPS = ((0, 1), (1, 1), (4, 2), (6, 2))
NEXT = (2, 3)
PLANE = tuple(
    sorted(
        ((dx, dy) for dx in range(NX) for dy in range(NY) if (dx, dy) != (0, 0)),
        key=lambda d: -(min(d[0], NX - d[0]) + min(d[1], NY - d[1])),
    )
)
MARGIN_CHUNKS = 16
DIRECT = 2
EARLY = 8
LATER = 8
MIDDLE = 5
NUM_SEMS = 192


def kernel(
    vox_in, phr_in, ids_in, mrg_in, vg_out, pg_out,
    vx, ph, idb, dt, st, ch, part, sb, rb, zs, zr, fs, fr, ms, mr, mo, vg, mrv, pg, fn, tb, ub,
    send_sem, recv_sem, loc_sem,
):
    rows, width = vox_in.shape
    own = phr_in.shape[0]
    half = width // 2
    scale = 1.0 / math.sqrt(width)
    b, c = lax.axis_index("batch"), lax.axis_index("crop")
    k, x, ylo, z = b % 2, (b // 2) % 4, (b // 8) % 2, b // 16
    y = c * 2 + ylo
    g, go = ylo * 4 + x, (1 - ylo) * 4 + x

    def at(dx=0, dy=0, dz=0, dk=0):
        xx, yy, zz, kk = (x + dx) % NX, (y + dy) % NY, (z + dz + NZ) % NZ, (k + dk) % 2
        return (((zz * 2 + yy % 2) * 4 + xx) * 2 + kk, yy // 2)

    count = [0]
    started = []

    def send(src, dst, where):
        n = count[0]
        count[0] += 1
        copy = pltpu.make_async_remote_copy(
            src_ref=src, dst_ref=dst, send_sem=send_sem.at[n], recv_sem=recv_sem.at[n],
            device_id=where, device_id_type=MESH,
        )
        copy.start()
        started.append(copy)
        return copy

    barrier = pltpu.get_barrier_semaphore()
    partners = [dict(dk=1)]
    partners += [dict(dz=o) for o in OFFS[1:]]
    partners += [dict(dx=dx, dy=dy) for dx, dy in PLANE]
    partners += [dict(dy=2, dz=dz) for dz in (2, -2, 3, -3, 4)]
    for p in partners:
        pl.semaphore_signal(barrier, inc=1, device_id=at(**p), device_id_type=MESH)

    mine = pl.ds(pl.multiple_of(k * rows, rows), rows)
    load_vox = pltpu.make_async_copy(vox_in, vx.at[mine], loc_sem.at[0])
    load_vox.start()
    load_phr = pltpu.make_async_copy(phr_in, ph.at[0, g], loc_sem.at[1])
    load_phr.start()
    load_ids = pltpu.make_async_copy(ids_in, idb.at[g, 0], loc_sem.at[6])
    load_ids.start()
    load_mrg = pltpu.make_async_copy(mrg_in, mrv, loc_sem.at[7])
    load_mrg.start()
    pl.semaphore_wait(barrier, len(partners))

    margin = []
    step = ch.shape[0] // MARGIN_CHUNKS

    def send_margin(n):
        for _ in range(n):
            i = len(margin)
            if i < MARGIN_CHUNKS:
                piece = pl.ds(i * step, step)
                margin.append(send(ch.at[piece], part.at[piece], at(dy=2)))

    def forward(n, start, which):
        return [
            send(ph.at[pl.ds(start, n), which], ph.at[pl.ds(start, n), which], at(dx=dx))
            for dx in (2, 1, 3)
        ]

    def across(n, start):
        lo, hi = pl.ds(0, half), pl.ds(half, half)
        s = pl.ds(start, n)
        return [
            send(ph.at[s, g, :, lo], ph.at[s, g, :, lo], at(dy=1)),
            send(ph.at[s, g, :, hi], ph.at[s, g, :, hi], at(dy=3)),
        ]

    def direct(n, start):
        lo, hi = pl.ds(0, half), pl.ds(half, half)
        s = pl.ds(start, n)
        copies = []
        for dx in (2, 1, 3, 0):
            copies.append(send(ph.at[s, g, :, lo], ph.at[s, g, :, lo], at(dx=dx, dy=1)))
            copies.append(send(ph.at[s, g, :, hi], ph.at[s, g, :, hi], at(dx=dx, dy=3)))
        return copies

    zc = {}
    idc = {p: send(ids_in, idb.at[g, BACK[p]], at(dz=OFFS[p])) for p in range(1, NZ)}
    for p in (5, 4, 7, 6, 1):
        zc[p] = send(phr_in, ph.at[BACK[p], g], at(dz=OFFS[p]))
    same, other, cross = [], [], {}
    load_phr.wait()
    other.append(direct(1, 0))
    same.append(forward(1, 0, g))
    swap_vox = send(vox_in, vx.at[mine], at(dk=1))
    load_mrg.wait()
    st[...] = (lax.broadcasted_iota(jnp.int32, st.shape, 0) == mrv[...]).astype(F32).astype(BF16)
    load_vox.wait()
    ch[...] = lax.dot_general(st[...], vx[mine, :], TN, preferred_element_type=F32).astype(BF16)
    load_ids.wait()

    def relay(i):
        start, n = GROUPS[i]
        for q in range(start, start + n):
            zc[BACK[q]].wait_recv()
        if i < DIRECT:
            other.append(direct(n, start))
        else:
            cross[i] = across(n, start)
        same.append(forward(n, start, g))

    def relay_other(i):
        start, n = GROUPS[i]
        for copy in cross[i]:
            copy.wait_recv()
        other.append(forward(n, start, go))

    send_margin(EARLY)
    relay(1)
    for p in range(1, NZ):
        idc[p].wait_recv()
    beside = 1 + 2 * ylo
    ids_seen = [send(idb.at[g], idb.at[g], at(dx=dx, dy=beside)) for dx in (2, 1, 3, 0)]
    ids_seen += [send(idb.at[g], idb.at[g], at(dx=dx)) for dx in (2, 1, 3)]
    relay(2)
    for copy in same[0] + other[0]:
        copy.wait_recv()
    slabs = [send(ph.at[0], ph.at[BACK[p]], at(dz=OFFS[p])) for p in NEXT]
    relay(3)
    send_margin(LATER)
    relay_other(2)

    chunk = 1024
    total = vx.shape[0]
    first_vol = (b // 2) * (total // VOX_VOL)
    lane = lax.broadcasted_iota(jnp.int32, (128, own), 1)
    row16 = lax.broadcasted_iota(jnp.int32, (128, own), 0) % own
    pick = lane == row16

    def logits(i):
        for copy in arrivals[i]:
            copy.wait_recv()
        block = ph[2 * i : 2 * i + 2].reshape(256, width)
        cols = []
        for j in range(2):
            ids = jnp.broadcast_to(idb[:, 2 * i + j], (8, own, own)).reshape(128, own)
            cols.append(jnp.sum(jnp.where(pick, ids, 0).astype(F32), axis=1, keepdims=True))
        ids = jnp.concatenate(cols, axis=0)
        for t in range(total // chunk):
            c0 = t * chunk
            acc = lax.dot_general(block, vx[c0 : c0 + chunk, :], NT, preferred_element_type=F32)
            logit = acc * scale - 1.0
            vol = first_vol + (c0 + lax.broadcasted_iota(jnp.int32, (1, chunk), 1)) // VOX_VOL
            match = ids == vol.astype(F32)
            r = 1.0 / (1.0 + jnp.exp(jnp.where(match, logit, -logit)))
            dt[i * 256 : (i + 1) * 256, c0 : c0 + chunk] = jnp.where(match, -r, r).astype(BF16)

    pieces = {}

    def terms(i):
        r = jnp.dot(dt[i * 256 : (i + 1) * 256, :], vx[...], preferred_element_type=F32)
        for gg in range(8):
            for h in range(2):
                for j in range(2):
                    r0 = j * 128 + gg * own
                    tile = r[r0 : r0 + own, h * half : (h + 1) * half]
                    if i == 0 and j == 0:
                        tile = tile + ub[0, gg, h].astype(F32) + ub[1, gg, h].astype(F32)
                    if i == 1:
                        tb[j, gg, h] = tile.astype(BF16)
                    else:
                        sb[i, gg, h, j] = tile.astype(BF16)

    def send_terms(i):
        copies = []
        for n, (dx, dy) in enumerate(PLANE):
            yy = (y + dy) % NY
            gg = (yy % 2) * 4 + (x + dx) % NX
            copies.append(send(sb.at[i, gg, yy // 2], rb.at[i, n], at(dx=dx, dy=dy)))
        pieces[i] = copies

    zsum, near = {}, {}

    def collect(i):
        for copy in pieces[i]:
            copy.wait_recv()
        acc = sb[i, g, c].astype(F32)
        for n in range(len(PLANE)):
            acc = acc + rb[i, n].astype(F32)
        zs[2 * i : 2 * i + 2] = acc
        for p in (2 * i, 2 * i + 1):
            if p:
                zsum[p] = send(zs.at[p], zr.at[BACK[p]], at(dz=OFFS[p]))
                near[p] = send(zs.at[p], fn.at[BACK[p]], at(dy=2, dz=OFFS[p]))

    swap_vox.wait_recv()
    for copy in ids_seen:
        copy.wait_recv()
    send_margin(MIDDLE)
    arrivals = {0: same[1] + other[1], 1: slabs, 2: same[2] + other[2], 3: list(same[3])}
    logits(0)
    relay_other(3)
    send_margin(MARGIN_CHUNKS)
    arrivals[3] += other[3]
    logits(1)
    terms(1)
    slabs_back = [send(tb.at[j], ub.at[j], at(dz=OFFS[p])) for j, p in enumerate(NEXT)]
    logits(2)
    terms(2)
    send_terms(2)
    logits(3)
    terms(3)
    send_terms(3)
    for copy in slabs_back:
        copy.wait_recv()
    terms(0)
    send_terms(0)

    flat = ph[...].reshape(NZ * 128, width)
    mstep = 512
    swaps = []
    for t in range(rows // mstep):
        cols = pl.ds(pl.multiple_of((1 - k) * rows + t * mstep, mstep), mstep)
        piece = pl.ds(t * mstep, mstep)
        ms[piece, :] = lax.dot_general(dt[:, cols], flat, TN, preferred_element_type=F32)
    for t in range(rows // mstep):
        piece = pl.ds(t * mstep, mstep)
        swaps.append(send(ms.at[piece], mr.at[piece], at(dk=1)))
    collect(2)
    for t in range(rows // mstep):
        cols = pl.ds(pl.multiple_of(k * rows + t * mstep, mstep), mstep)
        piece = pl.ds(t * mstep, mstep)
        mo[piece, :] = lax.dot_general(dt[:, cols], flat, TN, preferred_element_type=F32)
    collect(3)
    collect(0)
    fs[...] = zs[0]
    last = send(fs, fr, at(dy=2))
    for copy in margin:
        copy.wait_recv()
    for copy in swaps:
        copy.wait_recv()
    fstep = 256
    stores = []
    for t in range(rows // fstep):
        piece = pl.ds(t * fstep, fstep)
        sel = st[piece, :]
        held = jnp.sum(sel.astype(F32), axis=1, keepdims=True)
        lower = pl.ds(pl.multiple_of(k * rows + t * fstep, fstep), fstep)
        extra = vx[lower, :].astype(F32) * held - jnp.dot(sel, part[...], preferred_element_type=F32)
        vg[piece, :] = (mo[piece, :] + mr[piece, :]) * scale + extra
    for t in range(rows // fstep):
        piece = pl.ds(t * fstep, fstep)
        store = pltpu.make_async_copy(vg.at[piece], vg_out.at[piece], loc_sem.at[2 + t])
        store.start()
        stores.append(store)
    acc, rest = zs[0], jnp.zeros_like(zs[0])
    for p in (5, 4, 7, 6, 1):
        zsum[p].wait_recv()
        near[p].wait_recv()
        acc = acc + zr[BACK[p]]
        rest = rest + fn[BACK[p]]
    last.wait_recv()
    a, d = acc * scale, (fr[...] + rest) * scale
    pg[:, 0:half] = jnp.where(c == 0, a, d)
    pg[:, half:width] = jnp.where(c == 0, d, a)
    store = pltpu.make_async_copy(pg, pg_out, loc_sem.at[8])
    store.start()
    for copy in stores + [store]:
        copy.wait()
    for copy in started:
        copy.wait_send()
    assert count[0] <= NUM_SEMS


def local(voxels, phrases, pair_ids, margin_index):
    rows, width = voxels.shape[1:]
    own = phrases.shape[0]
    ovl = margin_index.shape[-1]
    half = width // 2
    hbm = pl.BlockSpec(memory_space=pltpu.HBM)
    any_space = pl.BlockSpec(memory_space=pl.ANY)
    inputs = (voxels[0], phrases, pair_ids[None], margin_index[0])
    voxel_grad, phrase_grad = pl.pallas_call(
        kernel,
        name="grounding",
        out_shape=(
            jax.ShapeDtypeStruct((rows, width), F32),
            jax.ShapeDtypeStruct((own, width), F32),
        ),
        in_specs=[hbm, hbm, hbm, hbm],
        out_specs=(any_space, any_space),
        scratch_shapes=[
            pltpu.VMEM((2 * rows, width), BF16),
            pltpu.VMEM((NZ, 8, own, width), BF16),
            pltpu.VMEM((8, NZ, 1, own), jnp.int32),
            pltpu.VMEM((NZ * 8 * own, 2 * rows), BF16),
            pltpu.VMEM((rows, ovl), BF16),
            pltpu.VMEM((ovl, width), BF16),
            pltpu.VMEM((ovl, width), BF16),
            pltpu.VMEM((4, 8, 2, 2, own, half), BF16),
            pltpu.VMEM((4, 15, 2, own, half), BF16),
            pltpu.VMEM((NZ, own, half), F32),
            pltpu.VMEM((NZ, own, half), F32),
            pltpu.VMEM((own, half), F32),
            pltpu.VMEM((own, half), F32),
            pltpu.VMEM((rows, width), F32),
            pltpu.VMEM((rows, width), F32),
            pltpu.VMEM((rows, width), F32),
            pltpu.VMEM((rows, width), F32),
            pltpu.VMEM((1, ovl), jnp.int32),
            pltpu.VMEM((own, width), F32),
            pltpu.VMEM((NZ, own, half), F32),
            pltpu.VMEM((2, 8, 2, own, half), BF16),
            pltpu.VMEM((2, 8, 2, own, half), BF16),
            pltpu.SemaphoreType.DMA((NUM_SEMS,)),
            pltpu.SemaphoreType.DMA((NUM_SEMS,)),
            pltpu.SemaphoreType.DMA((16,)),
        ],
        compiler_params=pltpu.CompilerParams(
            collective_id=0, has_side_effects=True, vmem_limit_bytes=24 * 2**20
        ),
    )(*(pltpu.with_memory_space_constraint(a, pltpu.HBM) for a in inputs))
    return (voxel_grad[None], phrase_grad)


def solution(mesh):
    placed = (P("crop", "batch", None), P("batch", None), P("batch"), P("crop", "batch", None))
    return jax.shard_map(
        local,
        mesh=mesh,
        in_specs=placed,
        out_specs=(P("crop", "batch", None), P("batch", None)),
        check_vma=False,
    )
```

```python
import math

import jax
import jax.numpy as jnp
from jax import lax
from jax.experimental import pallas as pl
from jax.experimental.pallas import tpu as pltpu
from jax.sharding import PartitionSpec as P

MESH = pl.DeviceIdType.MESH
F32, BF16 = jnp.float32, jnp.bfloat16
NT = (((1,), (1,)), ((), ()))
TN = (((0,), (0,)), ((), ()))
VOX_VOL = 256
NX, NY, NZ = 4, 4, 8
OFFS = (0, -2, 1, -1, 3, 4, 2, -3)
BACK = tuple(OFFS.index(-o if o != 4 else 4) for o in OFFS)
GROUPS = ((0, 1), (1, 1), (4, 2), (6, 2))
NEXT = (2, 3)
NEAR = (1, 6, 7)
PLANE = tuple(
    sorted(
        ((dx, dy) for dx in range(NX) for dy in range(NY) if (dx, dy) != (0, 0)),
        key=lambda d: -(min(d[0], NX - d[0]) + min(d[1], NY - d[1])),
    )
)
MARGIN_CHUNKS = 16
DIRECT = 2
EARLY = 7
LATER = 9
NUM_SEMS = 192


def encode(v):
    return (v * jnp.abs(v)).astype(BF16)


def decode(w):
    w = w.astype(F32)
    root = jnp.sqrt(jnp.abs(w))
    return jnp.where(w < 0, -root, root)


def kernel(
    vox_in, phr_in, ids_in, mrg_in, vg_out, pg_out,
    vx, ph, idb, dt, st, ch, part, sb, rb, zs, zr, fs, fr, ms, mr, mo, vg, mrv, pg, fn, tb, ub,
    send_sem, recv_sem, loc_sem,
):
    rows, width = vox_in.shape
    own = phr_in.shape[0]
    half = width // 2
    scale = 1.0 / math.sqrt(width)
    b, c = lax.axis_index("batch"), lax.axis_index("crop")
    k, x, ylo, z = b % 2, (b // 2) % 4, (b // 8) % 2, b // 16
    y = c * 2 + ylo
    g, go = ylo * 4 + x, (1 - ylo) * 4 + x

    def at(dx=0, dy=0, dz=0, dk=0):
        xx, yy, zz, kk = (x + dx) % NX, (y + dy) % NY, (z + dz + NZ) % NZ, (k + dk) % 2
        return (((zz * 2 + yy % 2) * 4 + xx) * 2 + kk, yy // 2)

    count = [0]
    started = []

    def send(src, dst, where):
        n = count[0]
        count[0] += 1
        copy = pltpu.make_async_remote_copy(
            src_ref=src, dst_ref=dst, send_sem=send_sem.at[n], recv_sem=recv_sem.at[n],
            device_id=where, device_id_type=MESH,
        )
        copy.start()
        started.append(copy)
        return copy

    barrier = pltpu.get_barrier_semaphore()
    partners = [dict(dk=1)]
    partners += [dict(dz=o) for o in OFFS[1:]]
    partners += [dict(dx=dx, dy=dy) for dx, dy in PLANE]
    partners += [dict(dy=2, dz=dz) for dz in (2, -2, 3, -3)]
    for p in partners:
        pl.semaphore_signal(barrier, inc=1, device_id=at(**p), device_id_type=MESH)

    mine = pl.ds(pl.multiple_of(k * rows, rows), rows)
    load_vox = pltpu.make_async_copy(vox_in, vx.at[mine], loc_sem.at[0])
    load_vox.start()
    load_phr = pltpu.make_async_copy(phr_in, ph.at[0, g], loc_sem.at[1])
    load_phr.start()
    load_ids = pltpu.make_async_copy(ids_in, idb.at[g, 0], loc_sem.at[6])
    load_ids.start()
    load_mrg = pltpu.make_async_copy(mrg_in, mrv, loc_sem.at[7])
    load_mrg.start()
    pl.semaphore_wait(barrier, len(partners))

    margin = []
    step = ch.shape[0] // MARGIN_CHUNKS

    def send_margin(n):
        for _ in range(n):
            i = len(margin)
            if i < MARGIN_CHUNKS:
                piece = pl.ds(i * step, step)
                margin.append(send(ch.at[piece], part.at[piece], at(dy=2)))

    def forward(n, start, which):
        return [
            send(ph.at[pl.ds(start, n), which], ph.at[pl.ds(start, n), which], at(dx=dx))
            for dx in (2, 1, 3)
        ]

    def across(n, start):
        lo, hi = pl.ds(0, half), pl.ds(half, half)
        s = pl.ds(start, n)
        return [
            send(ph.at[s, g, :, lo], ph.at[s, g, :, lo], at(dy=1)),
            send(ph.at[s, g, :, hi], ph.at[s, g, :, hi], at(dy=3)),
        ]

    def direct(n, start):
        lo, hi = pl.ds(0, half), pl.ds(half, half)
        s = pl.ds(start, n)
        copies = []
        for dx in (2, 1, 3, 0):
            copies.append(send(ph.at[s, g, :, lo], ph.at[s, g, :, lo], at(dx=dx, dy=1)))
            copies.append(send(ph.at[s, g, :, hi], ph.at[s, g, :, hi], at(dx=dx, dy=3)))
        return copies

    zc = {}
    idc = {p: send(ids_in, idb.at[g, BACK[p]], at(dz=OFFS[p])) for p in range(1, NZ)}
    for p in (1, 5, 4, 7, 6):
        zc[p] = send(phr_in, ph.at[BACK[p], g], at(dz=OFFS[p]))
    same, other, cross = [], [], {}
    load_phr.wait()
    other.append(direct(1, 0))
    same.append(forward(1, 0, g))
    swap_vox = send(vox_in, vx.at[mine], at(dk=1))
    load_mrg.wait()
    st[...] = (lax.broadcasted_iota(jnp.int32, st.shape, 0) == mrv[...]).astype(F32).astype(BF16)
    load_vox.wait()
    ch[...] = lax.dot_general(st[...], vx[mine, :], TN, preferred_element_type=F32).astype(BF16)
    load_ids.wait()

    def relay(i):
        start, n = GROUPS[i]
        for q in range(start, start + n):
            zc[BACK[q]].wait_recv()
        if i < DIRECT:
            other.append(direct(n, start))
        else:
            cross[i] = across(n, start)
        same.append(forward(n, start, g))

    def relay_other(i):
        start, n = GROUPS[i]
        for copy in cross[i]:
            copy.wait_recv()
        other.append(forward(n, start, go))

    send_margin(EARLY)
    relay(1)
    for p in range(1, NZ):
        idc[p].wait_recv()
    beside = 1 + 2 * ylo
    ids_seen = [send(idb.at[g], idb.at[g], at(dx=dx, dy=beside)) for dx in (2, 1, 3, 0)]
    ids_seen += [send(idb.at[g], idb.at[g], at(dx=dx)) for dx in (2, 1, 3)]
    relay(2)
    for copy in same[0] + other[0]:
        copy.wait_recv()
    slabs = [send(ph.at[0], ph.at[BACK[p]], at(dz=OFFS[p])) for p in NEXT]
    relay(3)
    send_margin(LATER)

    chunk = 1024
    total = vx.shape[0]
    first_vol = (b // 2) * (total // VOX_VOL)
    lane = lax.broadcasted_iota(jnp.int32, (128, own), 1)
    row16 = lax.broadcasted_iota(jnp.int32, (128, own), 0) % own
    pick = lane == row16

    def logits(i):
        for copy in arrivals[i]:
            copy.wait_recv()
        block = ph[2 * i : 2 * i + 2].reshape(256, width)
        cols = []
        for j in range(2):
            ids = jnp.broadcast_to(idb[:, 2 * i + j], (8, own, own)).reshape(128, own)
            cols.append(jnp.sum(jnp.where(pick, ids, 0).astype(F32), axis=1, keepdims=True))
        ids = jnp.concatenate(cols, axis=0)
        for t in range(total // chunk):
            c0 = t * chunk
            acc = lax.dot_general(block, vx[c0 : c0 + chunk, :], NT, preferred_element_type=F32)
            logit = acc * scale - 1.0
            vol = first_vol + (c0 + lax.broadcasted_iota(jnp.int32, (1, chunk), 1)) // VOX_VOL
            match = ids == vol.astype(F32)
            r = 1.0 / (1.0 + jnp.exp(jnp.where(match, logit, -logit)))
            dt[i * 256 : (i + 1) * 256, c0 : c0 + chunk] = jnp.where(match, -r, r).astype(BF16)

    pieces = {}

    def terms(i):
        r = jnp.dot(dt[i * 256 : (i + 1) * 256, :], vx[...], preferred_element_type=F32)
        for gg in range(8):
            for h in range(2):
                for j in range(2):
                    r0 = j * 128 + gg * own
                    tile = r[r0 : r0 + own, h * half : (h + 1) * half]
                    if i == 0 and j == 0:
                        tile = tile + decode(ub[0, gg, h]) + decode(ub[1, gg, h])
                    if i == 1:
                        tb[j, gg, h] = encode(tile)
                    else:
                        sb[i, gg, h, j] = encode(tile)

    def send_terms(i):
        copies = []
        for n, (dx, dy) in enumerate(PLANE):
            yy = (y + dy) % NY
            gg = (yy % 2) * 4 + (x + dx) % NX
            copies.append(send(sb.at[i, gg, yy // 2], rb.at[i, n], at(dx=dx, dy=dy)))
        pieces[i] = copies

    zsum, near = {}, {}

    def collect(i):
        for copy in pieces[i]:
            copy.wait_recv()
        acc = decode(sb[i, g, c])
        for n in range(len(PLANE)):
            acc = acc + decode(rb[i, n])
        zs[2 * i : 2 * i + 2] = acc
        for p in (2 * i, 2 * i + 1):
            if p:
                zsum[p] = send(zs.at[p], zr.at[BACK[p]], at(dz=OFFS[p]))
            if p in NEAR:
                near[p] = send(zs.at[p], fn.at[BACK[p]], at(dy=2, dz=OFFS[p]))

    swap_vox.wait_recv()
    for copy in ids_seen:
        copy.wait_recv()
    arrivals = {0: same[1] + other[1], 1: slabs}
    logits(0)
    relay_other(2)
    relay_other(3)
    arrivals[2], arrivals[3] = same[2] + other[2], same[3] + other[3]
    logits(1)
    terms(1)
    slabs_back = [send(tb.at[j], ub.at[j], at(dz=OFFS[p])) for j, p in enumerate(NEXT)]
    logits(2)
    terms(2)
    send_terms(2)
    logits(3)
    terms(3)
    send_terms(3)
    for copy in slabs_back:
        copy.wait_recv()
    terms(0)
    send_terms(0)

    flat = ph[...].reshape(NZ * 128, width)
    mstep = 512
    swaps = []
    for t in range(rows // mstep):
        cols = pl.ds(pl.multiple_of((1 - k) * rows + t * mstep, mstep), mstep)
        piece = pl.ds(t * mstep, mstep)
        ms[piece, :] = lax.dot_general(dt[:, cols], flat, TN, preferred_element_type=F32)
    for t in range(rows // mstep):
        piece = pl.ds(t * mstep, mstep)
        swaps.append(send(ms.at[piece], mr.at[piece], at(dk=1)))
    collect(2)
    for t in range(rows // mstep):
        cols = pl.ds(pl.multiple_of(k * rows + t * mstep, mstep), mstep)
        piece = pl.ds(t * mstep, mstep)
        mo[piece, :] = lax.dot_general(dt[:, cols], flat, TN, preferred_element_type=F32)
    collect(3)
    collect(0)
    acc = zs[0]
    for p in (5, 4):
        zsum[p].wait_recv()
        acc = acc + zr[BACK[p]]
    fs[...] = acc
    last = send(fs, fr, at(dy=2))
    for copy in margin:
        copy.wait_recv()
    for copy in swaps:
        copy.wait_recv()
    fstep = 256
    stores = []
    for t in range(rows // fstep):
        piece = pl.ds(t * fstep, fstep)
        sel = st[piece, :]
        held = jnp.sum(sel.astype(F32), axis=1, keepdims=True)
        lower = pl.ds(pl.multiple_of(k * rows + t * fstep, fstep), fstep)
        extra = vx[lower, :].astype(F32) * held - jnp.dot(sel, part[...], preferred_element_type=F32)
        vg[piece, :] = (mo[piece, :] + mr[piece, :]) * scale + extra
    for t in range(rows // fstep):
        piece = pl.ds(t * fstep, fstep)
        store = pltpu.make_async_copy(vg.at[piece], vg_out.at[piece], loc_sem.at[2 + t])
        store.start()
        stores.append(store)
    rest = jnp.zeros_like(acc)
    for p in (7, 6, 1):
        zsum[p].wait_recv()
        near[p].wait_recv()
        acc = acc + zr[BACK[p]]
        rest = rest + fn[BACK[p]]
    last.wait_recv()
    a, d = acc * scale, (fr[...] + rest) * scale
    pg[:, 0:half] = jnp.where(c == 0, a, d)
    pg[:, half:width] = jnp.where(c == 0, d, a)
    store = pltpu.make_async_copy(pg, pg_out, loc_sem.at[8])
    store.start()
    for copy in stores + [store]:
        copy.wait()
    for copy in started:
        copy.wait_send()
    assert count[0] <= NUM_SEMS


def local(voxels, phrases, pair_ids, margin_index):
    rows, width = voxels.shape[1:]
    own = phrases.shape[0]
    ovl = margin_index.shape[-1]
    half = width // 2
    hbm = pl.BlockSpec(memory_space=pltpu.HBM)
    any_space = pl.BlockSpec(memory_space=pl.ANY)
    inputs = (voxels[0], phrases, pair_ids[None], margin_index[0])
    voxel_grad, phrase_grad = pl.pallas_call(
        kernel,
        name="grounding",
        out_shape=(
            jax.ShapeDtypeStruct((rows, width), F32),
            jax.ShapeDtypeStruct((own, width), F32),
        ),
        in_specs=[hbm, hbm, hbm, hbm],
        out_specs=(any_space, any_space),
        scratch_shapes=[
            pltpu.VMEM((2 * rows, width), BF16),
            pltpu.VMEM((NZ, 8, own, width), BF16),
            pltpu.VMEM((8, NZ, 1, own), jnp.int32),
            pltpu.VMEM((NZ * 8 * own, 2 * rows), BF16),
            pltpu.VMEM((rows, ovl), BF16),
            pltpu.VMEM((ovl, width), BF16),
            pltpu.VMEM((ovl, width), BF16),
            pltpu.VMEM((4, 8, 2, 2, own, half), BF16),
            pltpu.VMEM((4, 15, 2, own, half), BF16),
            pltpu.VMEM((NZ, own, half), F32),
            pltpu.VMEM((NZ, own, half), F32),
            pltpu.VMEM((own, half), F32),
            pltpu.VMEM((own, half), F32),
            pltpu.VMEM((rows, width), F32),
            pltpu.VMEM((rows, width), F32),
            pltpu.VMEM((rows, width), F32),
            pltpu.VMEM((rows, width), F32),
            pltpu.VMEM((1, ovl), jnp.int32),
            pltpu.VMEM((own, width), F32),
            pltpu.VMEM((NZ, own, half), F32),
            pltpu.VMEM((2, 8, 2, own, half), BF16),
            pltpu.VMEM((2, 8, 2, own, half), BF16),
            pltpu.SemaphoreType.DMA((NUM_SEMS,)),
            pltpu.SemaphoreType.DMA((NUM_SEMS,)),
            pltpu.SemaphoreType.DMA((16,)),
        ],
        compiler_params=pltpu.CompilerParams(
            collective_id=0, has_side_effects=True, vmem_limit_bytes=24 * 2**20
        ),
    )(*(pltpu.with_memory_space_constraint(a, pltpu.HBM) for a in inputs))
    return (voxel_grad[None], phrase_grad)


def solution(mesh):
    placed = (P("crop", "batch", None), P("batch", None), P("batch"), P("crop", "batch", None))
    return jax.shard_map(
        local,
        mesh=mesh,
        in_specs=placed,
        out_specs=(P("crop", "batch", None), P("batch", None)),
        check_vma=False,
    )
```

```python
import math

import jax
import jax.numpy as jnp
from jax import lax
from jax.experimental import pallas as pl
from jax.experimental.pallas import tpu as pltpu
from jax.sharding import PartitionSpec as P

MESH = pl.DeviceIdType.MESH
F32, BF16 = jnp.float32, jnp.bfloat16
NT = (((1,), (1,)), ((), ()))
TN = (((0,), (0,)), ((), ()))
VOX_VOL = 256
NX, NY, NZ = 4, 4, 8
OFFS = (0, -2, 1, -1, 3, 4, 2, -3)
BACK = tuple(OFFS.index(-o if o != 4 else 4) for o in OFFS)
GROUPS = ((0, 1), (1, 1), (4, 2), (6, 2))
NEXT = (2, 3)
NEAR = (1, 6, 7)
PLANE = tuple(
    sorted(
        ((dx, dy) for dx in range(NX) for dy in range(NY) if (dx, dy) != (0, 0)),
        key=lambda d: -(min(d[0], NX - d[0]) + min(d[1], NY - d[1])),
    )
)
MARGIN_CHUNKS = 16
DIRECT = 2
EARLY = 6
LATER = 10
NUM_SEMS = 192


def encode(v):
    return (v * jnp.abs(v)).astype(BF16)


def decode(w):
    w = w.astype(F32)
    root = jnp.sqrt(jnp.abs(w))
    return jnp.where(w < 0, -root, root)


def kernel(
    vox_in, phr_in, ids_in, mrg_in, vg_out, pg_out,
    vx, ph, idb, dt, st, ch, part, sb, rb, zs, zr, fs, fr, ms, mr, mo, vg, mrv, pg, fn, tb, ub,
    send_sem, recv_sem, loc_sem,
):
    rows, width = vox_in.shape
    own = phr_in.shape[0]
    half = width // 2
    scale = 1.0 / math.sqrt(width)
    b, c = lax.axis_index("batch"), lax.axis_index("crop")
    k, x, ylo, z = b % 2, (b // 2) % 4, (b // 8) % 2, b // 16
    y = c * 2 + ylo
    g, go = ylo * 4 + x, (1 - ylo) * 4 + x

    def at(dx=0, dy=0, dz=0, dk=0):
        xx, yy, zz, kk = (x + dx) % NX, (y + dy) % NY, (z + dz + NZ) % NZ, (k + dk) % 2
        return (((zz * 2 + yy % 2) * 4 + xx) * 2 + kk, yy // 2)

    count = [0]
    started = []

    def send(src, dst, where):
        n = count[0]
        count[0] += 1
        copy = pltpu.make_async_remote_copy(
            src_ref=src, dst_ref=dst, send_sem=send_sem.at[n], recv_sem=recv_sem.at[n],
            device_id=where, device_id_type=MESH,
        )
        copy.start()
        started.append(copy)
        return copy

    barrier = pltpu.get_barrier_semaphore()
    partners = [dict(dk=1)]
    partners += [dict(dz=o) for o in OFFS[1:]]
    partners += [dict(dx=dx, dy=dy) for dx, dy in PLANE]
    partners += [dict(dy=2, dz=dz) for dz in (2, -2, 3, -3)]
    for p in partners:
        pl.semaphore_signal(barrier, inc=1, device_id=at(**p), device_id_type=MESH)

    mine = pl.ds(pl.multiple_of(k * rows, rows), rows)
    load_vox = pltpu.make_async_copy(vox_in, vx.at[mine], loc_sem.at[0])
    load_vox.start()
    load_phr = pltpu.make_async_copy(phr_in, ph.at[0, g], loc_sem.at[1])
    load_phr.start()
    load_ids = pltpu.make_async_copy(ids_in, idb.at[g, 0], loc_sem.at[6])
    load_ids.start()
    load_mrg = pltpu.make_async_copy(mrg_in, mrv, loc_sem.at[7])
    load_mrg.start()
    pl.semaphore_wait(barrier, len(partners))

    margin = []
    step = ch.shape[0] // MARGIN_CHUNKS

    def send_margin(n):
        for _ in range(n):
            i = len(margin)
            if i < MARGIN_CHUNKS:
                piece = pl.ds(i * step, step)
                margin.append(send(ch.at[piece], part.at[piece], at(dy=2)))

    def forward(n, start, which):
        return [
            send(ph.at[pl.ds(start, n), which], ph.at[pl.ds(start, n), which], at(dx=dx))
            for dx in (2, 1, 3)
        ]

    def across(n, start):
        lo, hi = pl.ds(0, half), pl.ds(half, half)
        s = pl.ds(start, n)
        return [
            send(ph.at[s, g, :, lo], ph.at[s, g, :, lo], at(dy=1)),
            send(ph.at[s, g, :, hi], ph.at[s, g, :, hi], at(dy=3)),
        ]

    def direct(n, start):
        lo, hi = pl.ds(0, half), pl.ds(half, half)
        s = pl.ds(start, n)
        copies = []
        for dx in (2, 1, 3, 0):
            copies.append(send(ph.at[s, g, :, lo], ph.at[s, g, :, lo], at(dx=dx, dy=1)))
            copies.append(send(ph.at[s, g, :, hi], ph.at[s, g, :, hi], at(dx=dx, dy=3)))
        return copies

    zc = {}
    idc = {p: send(ids_in, idb.at[g, BACK[p]], at(dz=OFFS[p])) for p in range(1, NZ)}
    for p in (1, 5, 4, 7, 6):
        zc[p] = send(phr_in, ph.at[BACK[p], g], at(dz=OFFS[p]))
    same, other, cross = [], [], {}
    load_phr.wait()
    other.append(direct(1, 0))
    same.append(forward(1, 0, g))
    swap_vox = send(vox_in, vx.at[mine], at(dk=1))
    load_mrg.wait()
    st[...] = (lax.broadcasted_iota(jnp.int32, st.shape, 0) == mrv[...]).astype(F32).astype(BF16)
    load_vox.wait()
    ch[...] = lax.dot_general(st[...], vx[mine, :], TN, preferred_element_type=F32).astype(BF16)
    load_ids.wait()

    def relay(i):
        start, n = GROUPS[i]
        for q in range(start, start + n):
            zc[BACK[q]].wait_recv()
        if i < DIRECT:
            other.append(direct(n, start))
        else:
            cross[i] = across(n, start)
        same.append(forward(n, start, g))

    def relay_other(i):
        start, n = GROUPS[i]
        for copy in cross[i]:
            copy.wait_recv()
        other.append(forward(n, start, go))

    send_margin(EARLY)
    relay(1)
    for p in range(1, NZ):
        idc[p].wait_recv()
    beside = 1 + 2 * ylo
    ids_seen = [send(idb.at[g], idb.at[g], at(dx=dx, dy=beside)) for dx in (2, 1, 3, 0)]
    ids_seen += [send(idb.at[g], idb.at[g], at(dx=dx)) for dx in (2, 1, 3)]
    relay(2)
    for copy in same[0] + other[0]:
        copy.wait_recv()
    slabs = [send(ph.at[0], ph.at[BACK[p]], at(dz=OFFS[p])) for p in NEXT]
    relay(3)
    send_margin(LATER)

    chunk = 1024
    total = vx.shape[0]
    first_vol = (b // 2) * (total // VOX_VOL)
    lane = lax.broadcasted_iota(jnp.int32, (128, own), 1)
    row16 = lax.broadcasted_iota(jnp.int32, (128, own), 0) % own
    pick = lane == row16

    def logits(i):
        for copy in arrivals[i]:
            copy.wait_recv()
        block = ph[2 * i : 2 * i + 2].reshape(256, width)
        cols = []
        for j in range(2):
            ids = jnp.broadcast_to(idb[:, 2 * i + j], (8, own, own)).reshape(128, own)
            cols.append(jnp.sum(jnp.where(pick, ids, 0).astype(F32), axis=1, keepdims=True))
        ids = jnp.concatenate(cols, axis=0)
        for t in range(total // chunk):
            c0 = t * chunk
            acc = lax.dot_general(block, vx[c0 : c0 + chunk, :], NT, preferred_element_type=F32)
            logit = acc * scale - 1.0
            vol = first_vol + (c0 + lax.broadcasted_iota(jnp.int32, (1, chunk), 1)) // VOX_VOL
            match = ids == vol.astype(F32)
            r = 1.0 / (1.0 + jnp.exp(jnp.where(match, logit, -logit)))
            dt[i * 256 : (i + 1) * 256, c0 : c0 + chunk] = jnp.where(match, -r, r).astype(BF16)

    pieces = {}

    def terms(i):
        r = jnp.dot(dt[i * 256 : (i + 1) * 256, :], vx[...], preferred_element_type=F32)
        for gg in range(8):
            for h in range(2):
                for j in range(2):
                    r0 = j * 128 + gg * own
                    tile = r[r0 : r0 + own, h * half : (h + 1) * half]
                    if i == 0 and j == 0:
                        tile = tile + decode(ub[0, gg, h]) + decode(ub[1, gg, h])
                    if i == 1:
                        tb[j, gg, h] = encode(tile)
                    else:
                        sb[i, gg, h, j] = encode(tile)

    def send_terms(i):
        copies = []
        for n, (dx, dy) in enumerate(PLANE):
            yy = (y + dy) % NY
            gg = (yy % 2) * 4 + (x + dx) % NX
            copies.append(send(sb.at[i, gg, yy // 2], rb.at[i, n], at(dx=dx, dy=dy)))
        pieces[i] = copies

    zsum, near = {}, {}

    def collect(i):
        for copy in pieces[i]:
            copy.wait_recv()
        acc = decode(sb[i, g, c])
        for n in range(len(PLANE)):
            acc = acc + decode(rb[i, n])
        zs[2 * i : 2 * i + 2] = acc
        for p in (2 * i, 2 * i + 1):
            if p:
                zsum[p] = send(zs.at[p], zr.at[BACK[p]], at(dz=OFFS[p]))
            if p in NEAR:
                near[p] = send(zs.at[p], fn.at[BACK[p]], at(dy=2, dz=OFFS[p]))

    swap_vox.wait_recv()
    for copy in ids_seen:
        copy.wait_recv()
    arrivals = {0: same[1] + other[1], 1: slabs}
    logits(0)
    relay_other(2)
    relay_other(3)
    arrivals[2], arrivals[3] = same[2] + other[2], same[3] + other[3]
    logits(1)
    terms(1)
    slabs_back = [send(tb.at[j], ub.at[j], at(dz=OFFS[p])) for j, p in enumerate(NEXT)]
    logits(2)
    terms(2)
    send_terms(2)
    logits(3)
    terms(3)
    send_terms(3)
    for copy in slabs_back:
        copy.wait_recv()
    terms(0)
    send_terms(0)

    flat = ph[...].reshape(NZ * 128, width)
    mstep = 512
    swaps = []
    for t in range(rows // mstep):
        cols = pl.ds(pl.multiple_of((1 - k) * rows + t * mstep, mstep), mstep)
        piece = pl.ds(t * mstep, mstep)
        ms[piece, :] = lax.dot_general(dt[:, cols], flat, TN, preferred_element_type=F32)
    for t in range(rows // mstep):
        piece = pl.ds(t * mstep, mstep)
        swaps.append(send(ms.at[piece], mr.at[piece], at(dk=1)))
    collect(2)
    for t in range(rows // mstep):
        cols = pl.ds(pl.multiple_of(k * rows + t * mstep, mstep), mstep)
        piece = pl.ds(t * mstep, mstep)
        mo[piece, :] = lax.dot_general(dt[:, cols], flat, TN, preferred_element_type=F32)
    collect(3)
    collect(0)
    acc = zs[0]
    for p in (5, 4):
        zsum[p].wait_recv()
        acc = acc + zr[BACK[p]]
    fs[...] = acc
    last = send(fs, fr, at(dy=2))
    for copy in margin:
        copy.wait_recv()
    for copy in swaps:
        copy.wait_recv()
    fstep = 256
    stores = []
    for t in range(rows // fstep):
        piece = pl.ds(t * fstep, fstep)
        sel = st[piece, :]
        held = jnp.sum(sel.astype(F32), axis=1, keepdims=True)
        lower = pl.ds(pl.multiple_of(k * rows + t * fstep, fstep), fstep)
        extra = vx[lower, :].astype(F32) * held - jnp.dot(sel, part[...], preferred_element_type=F32)
        vg[piece, :] = (mo[piece, :] + mr[piece, :]) * scale + extra
    for t in range(rows // fstep):
        piece = pl.ds(t * fstep, fstep)
        store = pltpu.make_async_copy(vg.at[piece], vg_out.at[piece], loc_sem.at[2 + t])
        store.start()
        stores.append(store)
    rest = jnp.zeros_like(acc)
    for p in (7, 6, 1):
        zsum[p].wait_recv()
        near[p].wait_recv()
        acc = acc + zr[BACK[p]]
        rest = rest + fn[BACK[p]]
    last.wait_recv()
    a, d = acc * scale, (fr[...] + rest) * scale
    pg[:, 0:half] = jnp.where(c == 0, a, d)
    pg[:, half:width] = jnp.where(c == 0, d, a)
    store = pltpu.make_async_copy(pg, pg_out, loc_sem.at[8])
    store.start()
    for copy in stores + [store]:
        copy.wait()
    for copy in started:
        copy.wait_send()
    assert count[0] <= NUM_SEMS


def local(voxels, phrases, pair_ids, margin_index):
    rows, width = voxels.shape[1:]
    own = phrases.shape[0]
    ovl = margin_index.shape[-1]
    half = width // 2
    hbm = pl.BlockSpec(memory_space=pltpu.HBM)
    any_space = pl.BlockSpec(memory_space=pl.ANY)
    inputs = (voxels[0], phrases, pair_ids[None], margin_index[0])
    voxel_grad, phrase_grad = pl.pallas_call(
        kernel,
        name="grounding",
        out_shape=(
            jax.ShapeDtypeStruct((rows, width), F32),
            jax.ShapeDtypeStruct((own, width), F32),
        ),
        in_specs=[hbm, hbm, hbm, hbm],
        out_specs=(any_space, any_space),
        scratch_shapes=[
            pltpu.VMEM((2 * rows, width), BF16),
            pltpu.VMEM((NZ, 8, own, width), BF16),
            pltpu.VMEM((8, NZ, 1, own), jnp.int32),
            pltpu.VMEM((NZ * 8 * own, 2 * rows), BF16),
            pltpu.VMEM((rows, ovl), BF16),
            pltpu.VMEM((ovl, width), BF16),
            pltpu.VMEM((ovl, width), BF16),
            pltpu.VMEM((4, 8, 2, 2, own, half), BF16),
            pltpu.VMEM((4, 15, 2, own, half), BF16),
            pltpu.VMEM((NZ, own, half), F32),
            pltpu.VMEM((NZ, own, half), F32),
            pltpu.VMEM((own, half), F32),
            pltpu.VMEM((own, half), F32),
            pltpu.VMEM((rows, width), F32),
            pltpu.VMEM((rows, width), F32),
            pltpu.VMEM((rows, width), F32),
            pltpu.VMEM((rows, width), F32),
            pltpu.VMEM((1, ovl), jnp.int32),
            pltpu.VMEM((own, width), F32),
            pltpu.VMEM((NZ, own, half), F32),
            pltpu.VMEM((2, 8, 2, own, half), BF16),
            pltpu.VMEM((2, 8, 2, own, half), BF16),
            pltpu.SemaphoreType.DMA((NUM_SEMS,)),
            pltpu.SemaphoreType.DMA((NUM_SEMS,)),
            pltpu.SemaphoreType.DMA((16,)),
        ],
        compiler_params=pltpu.CompilerParams(
            collective_id=0, has_side_effects=True, vmem_limit_bytes=24 * 2**20
        ),
    )(*(pltpu.with_memory_space_constraint(a, pltpu.HBM) for a in inputs))
    return (voxel_grad[None], phrase_grad)


def solution(mesh):
    placed = (P("crop", "batch", None), P("batch", None), P("batch"), P("crop", "batch", None))
    return jax.shard_map(
        local,
        mesh=mesh,
        in_specs=placed,
        out_specs=(P("crop", "batch", None), P("batch", None)),
        check_vma=False,
    )
```
